32 devices in a mesh: groups: 2 (over y), row: 8 (over z, core), col: 2 (over x).
Axes of the slice: x: 2, y: 2, z: 4, core: 2. Of those that a mesh axis runs over, the one named last changes fastest.
Arguments:
- nodes: bfloat16 [1024, 768], P(('groups', 'row')), parts along dimension 0, may hold values from -6 to 6
- chain_ids: int32 [1024], P(('groups', 'row')), parts along dimension 0, may hold values from 0 to 3, never falling along the last dimension, each value on 1 to 256 neighbouring positions
- residue_index: int32 [1024], P(('groups', 'row')), parts along dimension 0, may hold values from 0 to 63
- pad_mask: int32 [1024], P(('groups', 'row')), parts along dimension 0, may hold values from 0 to 1, as said below
- pairs: bfloat16 [64, 1024, 512], P(None, ('groups', 'row'), 'col'), parts along dimension 1, may hold values from -6 to 6
- node_gain: float32 [768], replicated, may hold values from 0.1 to 1.9
- w_qkv: bfloat16 [768, 2304], replicated, may hold values from -0.21875 to 0.21875
- w_out: bfloat16 [768, 768], replicated, may hold values from -0.4375 to 0.4375
- pair_gain: float32 [64], replicated, may hold values from 0.1 to 1.9
- w_bias_gate: bfloat16 [96, 64], replicated, may hold values from -0.75 to 0.75
- rel_table: float32 [48, 66], replicated, may hold values from -6 to 6
- w_edge: bfloat16 [64, 48], replicated, may hold values from -0.875 to 0.875
- edge_norm_gain: float32 [64], replicated, may hold values from 0.1 to 1.9
- w_mlp_in: bfloat16 [256, 64], replicated, may hold values from -0.75 to 0.75
- w_mlp_out: bfloat16 [64, 256], replicated, may hold values from -0.375 to 0.375
Outputs:
- node_update: bfloat16 [1024, 768], P(('groups', 'row')), parts along dimension 0
- pairs_out: bfloat16 [64, 1024, 512], P(None, ('groups', 'row'), 'col'), parts along dimension 1
The draws below stay inside these ranges and needn't reach their ends.
There are 2 independent parts, one for each index of `groups`. The reference program is written for one: setup_inputs(seed, part) draws one part's arguments, and reference() takes and returns one part's arrays. A program takes and returns all parts, laid end to end along the dimension named above; an argument that names none is the same for every part. Nothing has to cross between parts.
Inputs may be any that keep to these rules, and one draw needn't show every extreme that they name: `chain_ids`: non-decreasing along the residues; each chain holds at most 256 residues. `pad_mask`: 1 on a leading run of at least 256 residues and 0 on the rest, which holds at least one residue.
All inputs are finite; a program needn't handle non-finite values.
Results may differ from the reference program's by a relative error of at most 0.0087.
Values may be sent and summed in bfloat16 or wider, within the bound.
A program may use at most 64 MiB of HBM per device.

```python
import math
import jax
import jax.numpy as jnp
import numpy as np
from jax import lax

D = 768
H = 48
DH = 16
C = 64
FFE = 256
RELMAX = 32
N = 512
BINS = 66


def draw_pad_mask(key, part):
    length = jax.random.randint(key, (), N // 2, N)
    return (jnp.arange(N) < length).astype(jnp.int32)


def set_ends(array, stream_key, low, largest):
    index_at = [jax.random.randint(jax.random.fold_in(stream_key, axis), (), 0, length) for axis, length in enumerate(array.shape)]
    longest = array.shape.index(max(array.shape))
    neighbour = index_at[:longest] + [(index_at[longest] + 1) % array.shape[longest]] + index_at[longest + 1:]
    return array.at[tuple(index_at)].set(low).at[tuple(neighbour)].set(largest)


def block_levels(own_key, dims, pieces, smallest, largest):
    gain, own = 1.0, jax.random.fold_in(own_key, 6)
    for axis_at, blocks in pieces:
        draws = jnp.exp(jax.random.uniform(jax.random.fold_in(own, axis_at), (blocks,), jnp.float32, smallest / len(pieces), largest / len(pieces)))
        gain = gain * jnp.repeat(draws, dims[axis_at] // blocks).reshape([-1 if axis == axis_at else 1 for axis in range(len(dims))])
    return gain


def split_up(amount, total, bound, lean):
    portions = [(1 << 20) // math.isqrt(standing ** lean) + 1 for standing in range(2, amount + 1)]
    spare, holding = total - bound - (amount - 1), [1] * (amount - 1)
    while spare > 0:
        candidates = [i for i in range(amount - 1) if holding[i] < bound]
        mass, left = sum([portions[i] for i in candidates]), spare
        for i in candidates:
            more = min(bound - holding[i], max(1, left * portions[i] // mass), spare)
            holding[i] = holding[i] + more
            spare = spare - more
    return np.array([bound] + holding)


def ragged(own_key, amount, total, limit, slope):
    if amount == 2:
        one = jax.random.randint(own_key, (), max(1, total - limit), min(limit, total - 1) + 1)
        return jnp.stack([one, total - one])
    lengths = jnp.asarray(split_up(amount, total, limit, slope), jnp.int32)
    twos = (amount - 1) // 2
    giver, sink = lengths[1:1 + 2 * twos:2], lengths[2:2 + 2 * twos:2]
    room = jnp.minimum(giver - 1, limit - sink)
    passed = jax.random.randint(jax.random.fold_in(own_key, 1), (twos,), 0, 1 << 20) % (room + 1)
    lengths = lengths.at[1:1 + 2 * twos:2].set(giver - passed).at[2:2 + 2 * twos:2].set(sink + passed)
    return lengths[jax.random.permutation(jax.random.fold_in(own_key, 2), amount)]


def scatter_about(stream_key, dims, deviation, limit, shards=(), kind=jnp.bfloat16):
    level = block_levels(stream_key, dims, shards, -0.22, 0.18) if shards else 1.0
    array = jax.random.normal(stream_key, dims, jnp.float32) * deviation * level
    return jnp.minimum(jnp.maximum(array, -limit), limit).astype(kind)


def setup_inputs(seed: int = 0, part: int = 0) -> dict:
    seeds = jax.random.split(jax.random.key(seed), 16)
    part_splits = jax.random.split(jax.random.fold_in(seeds[15], part), 16)
    return {
        "nodes": scatter_about(part_splits[0], (N, D), 1.0, 6.0, ((0, 8),)),
        "chain_ids": jnp.searchsorted(jnp.cumsum(ragged(part_splits[1], 4, N, N // 2, 1)), jnp.arange(N), side="right").astype(jnp.int32),
        "residue_index": set_ends(jax.random.randint(part_splits[2], (N,), 0, 2 * RELMAX), jax.random.fold_in(part_splits[2], 1), 0, (2 * RELMAX) - 1).astype(jnp.int32),
        "pad_mask": draw_pad_mask(jax.random.fold_in(jax.random.fold_in(seeds[15], part), 71), part),
        "pairs": scatter_about(part_splits[4], (C, N, N), 1.0, 6.0, ((1, 8), (2, 2))),
        "node_gain": jnp.clip(1.0 + 0.18 * jax.random.normal(seeds[5], (D,), jnp.float32), 0.1, 1.9),
        "w_qkv": scatter_about(seeds[6], (D, 3 * D), D ** -0.5, 0.21875),
        "w_out": scatter_about(seeds[7], (D, D), (D // 4) ** -0.5, 0.4375),
        "pair_gain": jnp.clip(1.0 + 0.18 * jax.random.normal(seeds[8], (C,), jnp.float32), 0.1, 1.9),
        "w_bias_gate": scatter_about(seeds[9], (2 * H, C), C ** -0.5, 0.75),
        "rel_table": scatter_about(seeds[10], (H, BINS), 1.5, 6.0, (), jnp.float32),
        "w_edge": scatter_about(seeds[11], (C, H), H ** -0.5, 0.875),
        "edge_norm_gain": jnp.clip(1.0 + 0.18 * jax.random.normal(seeds[12], (C,), jnp.float32), 0.1, 1.9),
        "w_mlp_in": scatter_about(seeds[13], (FFE, C), C ** -0.5, 0.75),
        "w_mlp_out": scatter_about(seeds[14], (C, FFE), FFE ** -0.5, 0.375),
    }


def layer_norm(values, axis):
    mean = lax.optimization_barrier(jnp.mean(values, axis=axis, keepdims=True))
    var = lax.optimization_barrier(jnp.mean(jnp.square(values - mean), axis=axis, keepdims=True))
    return (values - mean) * lax.rsqrt(var + 1e-05)

def pair_block(zb, query_rows, key, value_rows, chain_r, res_r, chain_c, res_c, valid_c, pair_gain, w_bias_gate, rel_table, w_edge, edge_norm_gain, w_mlp_in, w_mlp_out):
    chans, nrow, ncol = zb.shape
    heads = rel_table.shape[0]
    zf = zb.astype(jnp.float32)
    pnorm = (layer_norm(zf, 0) * pair_gain[:, None, None]).astype(jnp.bfloat16)
    bias_gate = jnp.dot(w_bias_gate, pnorm.reshape(chans, nrow * ncol), preferred_element_type=jnp.float32).reshape(2 * heads, nrow, ncol)
    bias = bias_gate[:heads]
    gate = bias_gate[heads:]
    offset = jnp.clip(res_r[:, None] - res_c[None, :], -RELMAX, RELMAX) + RELMAX
    offset_classes = jnp.where(chain_r[:, None] == chain_c[None, :], offset, 2 * RELMAX + 1).astype(jnp.int32)
    rel = rel_table[:, offset_classes]
    score_logits = jnp.einsum('axt,zxt->xaz', query_rows.astype(jnp.float32), key.astype(jnp.float32))
    logits = jnp.clip(0.25 * score_logits + bias + rel, -5.0, 5.0)
    weights = jnp.where(valid_c[None, None, :], jnp.exp(logits), jnp.float32(0.0))
    gated_output = (weights * jax.nn.sigmoid(gate)).astype(jnp.bfloat16)
    numerator_rows = jnp.einsum('qby,yqo->bqo', gated_output.astype(jnp.float32), value_rows.astype(jnp.float32))
    denom = lax.optimization_barrier(jnp.sum(weights, axis=2))
    edge = jnp.dot(w_edge, logits.astype(jnp.bfloat16).reshape(heads, nrow * ncol), preferred_element_type=jnp.float32)
    first = zf.reshape(chans, nrow * ncol) + edge
    enorm = (layer_norm(first, 0) * edge_norm_gain[:, None]).astype(jnp.bfloat16)
    hidden = jax.nn.gelu(jnp.dot(w_mlp_in, enorm, preferred_element_type=jnp.float32)).astype(jnp.bfloat16)
    out = first + jnp.dot(w_mlp_out, hidden, preferred_element_type=jnp.float32)
    return (numerator_rows, denom, out.astype(jnp.bfloat16).reshape(chans, nrow, ncol))

def reference(nodes, chain_ids, residue_index, pad_mask, pairs, node_gain, w_qkv, w_out, pair_gain, w_bias_gate, rel_table, w_edge, edge_norm_gain, w_mlp_in, w_mlp_out):
    normed = (layer_norm(nodes.astype(jnp.float32), 1) * node_gain).astype(jnp.bfloat16)
    qkv = jnp.dot(normed, w_qkv, preferred_element_type=jnp.float32).astype(jnp.bfloat16)
    query_rows = qkv[:, :D].reshape(N, H, DH)
    key = qkv[:, D:2 * D].reshape(N, H, DH)
    value_rows = qkv[:, 2 * D:].reshape(N, H, DH)
    valid = pad_mask == 1
    block = 16 if N % 16 == 0 else N
    count = N // block

    def one(index):
        start = (index * block).astype(jnp.int32)
        zb = lax.dynamic_slice_in_dim(pairs, start, block, 1)
        qb = lax.dynamic_slice_in_dim(query_rows, start, block, 0)
        chain_r = lax.dynamic_slice_in_dim(chain_ids, start, block, 0)
        res_r = lax.dynamic_slice_in_dim(residue_index, start, block, 0)
        return pair_block(zb, qb, key, value_rows, chain_r, res_r, chain_ids, residue_index, valid, pair_gain, w_bias_gate, rel_table, w_edge, edge_norm_gain, w_mlp_in, w_mlp_out)
    numerator_rows, denom, outs = lax.map(one, jnp.arange(count, dtype=jnp.int32))
    numerator_rows = numerator_rows.reshape(N, H, DH)
    denom = jnp.transpose(denom, (0, 2, 1)).reshape(N, H)
    attended = (numerator_rows / denom[:, :, None]).reshape(N, D).astype(jnp.bfloat16)
    node_update = jnp.dot(attended, w_out, preferred_element_type=jnp.float32).astype(jnp.bfloat16)
    pairs_out = jnp.transpose(outs, (1, 0, 2, 3)).reshape(C, N, N)
    return (node_update, pairs_out)
```

```python
import functools
import jax
import jax.numpy as jnp
from jax import lax
from jax.experimental import pallas as pl
from jax.experimental.pallas import tpu as pltpu
from jax.sharding import PartitionSpec as P

IB = 16
SUB = 8
GELU_A = 2.0 * (2.0 / 3.141592653589793) ** 0.5
GELU_B = GELU_A * 4.0 * 0.044715


def node_norm(values, gain):
    mean = jnp.mean(values, axis=1, keepdims=True)
    var = jnp.mean(jnp.square(values - mean), axis=1, keepdims=True)
    return ((values - mean) * lax.rsqrt(var + 1e-05) * gain).astype(jnp.bfloat16)


def chan_norm(values, gain):
    inv = 1.0 / values.shape[0]
    mean = jnp.sum(values, axis=0, keepdims=True) * inv
    cent = values - mean
    var = jnp.sum(cent * cent, axis=0, keepdims=True) * inv
    return (cent * lax.rsqrt(var + 1e-05) * gain).astype(jnp.bfloat16)


def pair_kernel(
    radius,
    chain_r,
    res_r,
    pairs_ref,
    q_ref,
    kt_ref,
    v_ref,
    cols_ref,
    wcat_ref,
    pgain_ref,
    egain_ref,
    wedge_ref,
    win_ref,
    wout_ref,
    mask_ref,
    numer_ref,
    denom_ref,
    out_ref,
    zs,
    os,
    qb,
    gb,
):
    step = pl.program_id(0)
    chans, iblk, cols = pairs_ref.shape
    heads = wedge_ref.shape[1]
    cpad = (wcat_ref.shape[1] - chans) // 2
    lanes = 128
    nl = cols // lanes
    for t in range(nl):
        zs[t] = (
            pairs_ref[:, :, t * lanes : (t + 1) * lanes]
            .astype(jnp.float32)
            .reshape(chans * iblk, lanes)
        )
    chain_c = cols_ref[0:1, :]
    res_c = cols_ref[1:2, :]
    valid = (cols_ref[2:3, :] == 1).astype(jnp.float32)
    class_ids = lax.broadcasted_iota(jnp.int32, (cpad, cols), 0)

    @pl.when(step == 0)
    def _():
        denom_ref[...] = jnp.zeros_like(denom_ref)

    lane_ids = lax.broadcasted_iota(jnp.int32, denom_ref.shape, 1)

    def sub_block(s, carry):
        base = pl.multiple_of(s * SUB, SUB)
        for u in range(SUB):
            row = q_ref[pl.ds(base + u, 1), :]
            qb[u * heads : (u + 1) * heads, :] = (row * mask_ref[...]).astype(jnp.bfloat16)
        scores = jnp.dot(qb[...], kt_ref[...], preferred_element_type=jnp.float32)
        for u in range(SUB):
            i = base + u
            gi = step * iblk + i
            z = jnp.concatenate([zs[t, pl.ds(i, chans, stride=iblk), :] for t in range(nl)], axis=1)
            pnorm = chan_norm(z, pgain_ref[...])
            offset = jnp.clip(res_r[gi] - res_c, -radius, radius) + radius
            cls = jnp.where(chain_c == chain_r[gi], offset, 2 * radius + 1)
            hot = jnp.where(class_ids == cls, 1.0, 0.0).astype(jnp.bfloat16)
            rhs = jnp.concatenate([pnorm, hot, hot], axis=0)
            bias_gate = jnp.dot(wcat_ref[...], rhs, preferred_element_type=jnp.float32)
            logits = jnp.clip(
                scores[u * heads : (u + 1) * heads] + bias_gate[:heads], -5.0, 5.0
            )
            weights = jnp.exp(logits) * valid
            sig = 0.5 * jnp.tanh(0.5 * bias_gate[heads:]) + 0.5
            gb[u * heads : (u + 1) * heads, :] = (weights * sig).astype(jnp.bfloat16)
            dsum = jnp.sum(weights, axis=1, keepdims=True)
            denom_ref[...] = jnp.where(lane_ids == gi, dsum, denom_ref[...])
            first = z + jnp.dot(
                wedge_ref[...], logits.astype(jnp.bfloat16), preferred_element_type=jnp.float32
            )
            enorm = chan_norm(first, egain_ref[...])
            y = jnp.dot(win_ref[...], enorm, preferred_element_type=jnp.float32)
            arg = y * (GELU_A + GELU_B * (y * y))
            hidden = (y + y * jnp.tanh(arg)).astype(jnp.bfloat16)
            res = first + jnp.dot(wout_ref[...], hidden, preferred_element_type=jnp.float32)
            for t in range(nl):
                os[t, pl.ds(i, chans, stride=iblk), :] = res[:, t * lanes : (t + 1) * lanes]
        full = jnp.dot(gb[...], v_ref[...], preferred_element_type=jnp.float32)
        width = v_ref.shape[1]
        numer_ref[pl.ds(base, SUB), :] = jnp.sum(
            full.reshape(SUB, heads, width) * mask_ref[...][None], axis=1
        )
        return carry

    lax.fori_loop(0, iblk // SUB, sub_block, 0)
    for t in range(nl):
        out_ref[:, :, t * lanes : (t + 1) * lanes] = (
            os[t].reshape(chans, iblk, lanes).astype(jnp.bfloat16)
        )


def body(
    nodes,
    chain_ids,
    residue_index,
    pad_mask,
    pairs,
    node_gain,
    w_qkv,
    w_out,
    pair_gain,
    w_bias_gate,
    rel_table,
    w_edge,
    edge_norm_gain,
    w_mlp_in,
    w_mlp_out,
):
    rows, width = nodes.shape
    chans, _, cols = pairs.shape
    heads, classes = rel_table.shape
    head_size = width // heads
    radius = (classes - 2) // 2
    bf, f32 = jnp.bfloat16, jnp.float32
    col_start = lax.axis_index("col") * cols
    ints = jnp.stack([chain_ids, residue_index, pad_mask], axis=1).astype(bf)
    packed = jnp.concatenate([nodes, jnp.pad(ints, ((0, 0), (0, 125)))], axis=1)
    gathered = lax.all_gather(packed, "row", axis=0, tiled=True)
    own = node_norm(nodes.astype(f32), node_gain)
    query = 0.25 * jnp.dot(own, w_qkv[:, :width], preferred_element_type=f32).astype(bf).astype(f32)
    col_block = lax.dynamic_slice_in_dim(gathered, col_start, cols, 0)
    col_normed = node_norm(col_block[:, :width].astype(f32), node_gain)
    kt = lax.dot_general(
        w_qkv[:, width : 2 * width],
        col_normed,
        (((0,), (1,)), ((), ())),
        preferred_element_type=f32,
    ).astype(bf)
    value = jnp.dot(col_normed, w_qkv[:, 2 * width :], preferred_element_type=f32).astype(bf)
    col_ints = jnp.pad(col_block[:, width : width + 3].astype(jnp.int32).T, ((0, 5), (0, 0)))
    cpad = -(-classes // 16) * 16
    rel_hi = rel_table.astype(bf)
    rel_lo = (rel_table - lax.reduce_precision(rel_table, 8, 7)).astype(bf)
    grow = ((0, heads), (0, cpad - classes))
    wcat = jnp.concatenate([w_bias_gate, jnp.pad(rel_hi, grow), jnp.pad(rel_lo, grow)], axis=1)
    head_of = lax.broadcasted_iota(jnp.int32, (heads, width), 1) // head_size
    mask = (head_of == lax.broadcasted_iota(jnp.int32, (heads, width), 0)).astype(f32)
    dl = -(-rows // 128) * 128

    def fixed(shape):
        return pl.BlockSpec(shape, lambda i, *_: (0,) * len(shape))

    numer, denom, pairs_out = pl.pallas_call(
        functools.partial(pair_kernel, radius),
        grid_spec=pltpu.PrefetchScalarGridSpec(
            num_scalar_prefetch=2,
            grid=(rows // IB,),
            in_specs=[
                pl.BlockSpec((chans, IB, cols), lambda i, *_: (0, i, 0)),
                pl.BlockSpec((IB, width), lambda i, *_: (i, 0)),
                fixed((width, cols)),
                fixed((cols, width)),
                fixed((8, cols)),
                fixed(wcat.shape),
                fixed((chans, 1)),
                fixed((chans, 1)),
                fixed(w_edge.shape),
                fixed(w_mlp_in.shape),
                fixed(w_mlp_out.shape),
                fixed(mask.shape),
            ],
            out_specs=[
                pl.BlockSpec((IB, width), lambda i, *_: (i, 0)),
                fixed((heads, dl)),
                pl.BlockSpec((chans, IB, cols), lambda i, *_: (0, i, 0)),
            ],
            scratch_shapes=[
                pltpu.VMEM((cols // 128, chans * IB, 128), f32),
                pltpu.VMEM((cols // 128, chans * IB, 128), f32),
                pltpu.VMEM((SUB * heads, width), bf),
                pltpu.VMEM((SUB * heads, cols), bf),
            ],
        ),
        out_shape=[
            jax.ShapeDtypeStruct((rows, width), f32),
            jax.ShapeDtypeStruct((heads, dl), f32),
            jax.ShapeDtypeStruct((chans, rows, cols), bf),
        ],
        compiler_params=pltpu.CompilerParams(vmem_limit_bytes=48 << 20),
        name="pair_block",
    )(
        chain_ids,
        residue_index,
        pairs,
        query,
        kt,
        value,
        col_ints,
        wcat,
        pair_gain[:, None],
        edge_norm_gain[:, None],
        w_edge,
        0.5 * w_mlp_in,
        w_mlp_out,
        mask,
    )
    both = jnp.concatenate([numer, denom[:, :rows].T], axis=1)
    both = lax.psum(both, "col")
    attended = (
        (both[:, :width].reshape(rows, heads, head_size) / both[:, width:, None])
        .reshape(rows, width)
        .astype(bf)
    )
    node_update = jnp.dot(attended, w_out, preferred_element_type=f32).astype(bf)
    return (node_update, pairs_out)


def solution(mesh):
    split = P(("groups", "row"))
    in_specs = (
        P(("groups", "row"), None),
        split,
        split,
        split,
        P(None, ("groups", "row"), "col"),
    ) + (P(),) * 10
    out_specs = (P(("groups", "row"), None), P(None, ("groups", "row"), "col"))
    return jax.shard_map(body, mesh=mesh, in_specs=in_specs, out_specs=out_specs, check_vma=False)
```

```python
import functools
import jax
import jax.numpy as jnp
from jax import lax
from jax.experimental import pallas as pl
from jax.experimental.pallas import tpu as pltpu
from jax.sharding import PartitionSpec as P

IB = 16
NA = 4
NC = 8
ND = 4
GELU_A = 2.0 * (2.0 / 3.141592653589793) ** 0.5
GELU_B = GELU_A * 4.0 * 0.044715
MESH = pl.DeviceIdType.MESH
BF, F32 = jnp.bfloat16, jnp.float32
LANES = 128


def node_norm(values, gain):
    mean = jnp.mean(values, axis=1, keepdims=True)
    cent = values - mean
    var = jnp.mean(cent * cent, axis=1, keepdims=True)
    return (cent * lax.rsqrt(var + 1e-05) * gain).astype(BF)


def chan_norm(values, gain):
    inv = 1.0 / values.shape[0]
    mean = jnp.sum(values, axis=0, keepdims=True) * inv
    cent = values - mean
    var = jnp.sum(cent * cent, axis=0, keepdims=True) * inv
    return (cent * lax.rsqrt(var + 1e-05) * gain).astype(BF)


def column(row):
    n = row.shape[1]
    eye = lax.broadcasted_iota(jnp.int32, (n, n), 0) == lax.broadcasted_iota(jnp.int32, (n, n), 1)
    return jnp.sum(jnp.where(eye, row, 0.0), axis=1, keepdims=True)


def fused_kernel(
    nrow,
    ncol,
    chain_s,
    res_s,
    ints_ref,
    nodes_ref,
    pairs_hbm,
    wqkv_hbm,
    wo_hbm,
    ngain_ref,
    pgain_ref,
    egain_ref,
    wbg_ref,
    rel_ref,
    wedge_ref,
    win_ref,
    wout_ref,
    node_out,
    pairs_out,
    snd,
    rbuf,
    wqkv,
    wo,
    pin,
    pout,
    zs,
    os,
    bias_s,
    sig_s,
    lg_s,
    qf,
    key,
    val,
    qb,
    nd,
    xbuf,
    pin_sem,
    pout_sem,
    w_sem,
    dsend,
    fsend,
    recv,
    xsend,
    xrecv,
):
    rows, width = nodes_ref.shape
    chans = wbg_ref.shape[1]
    heads, classes = rel_ref.shape
    cols = key.shape[0]
    hsize = width // heads
    radius = (classes - 2) // 2
    npc = cols // rows
    nblk = rows // IB
    nl = cols // LANES
    half = nrow // 2
    r = lax.axis_index("row")
    c = lax.axis_index("col")
    par = lax.rem(r, 2)
    sib = r + 1 - 2 * par
    chip = r // 2
    slot = lax.rem(r, npc)
    is_src = r // npc == c

    def pair_in(b):
        return pltpu.make_async_copy(
            pairs_hbm.at[:, pl.ds(b * IB, IB), :], pin.at[b], pin_sem.at[b]
        )

    def pair_outc(b):
        return pltpu.make_async_copy(
            pout.at[b], pairs_out.at[:, pl.ds(b * IB, IB), :], pout_sem.at[b]
        )

    wq_copy = pltpu.make_async_copy(wqkv_hbm, wqkv, w_sem.at[0])
    wo_copy = pltpu.make_async_copy(wo_hbm, wo, w_sem.at[1])
    for b in range(nblk):
        pair_in(b).start()
    wq_copy.start()
    wo_copy.start()

    barrier = pltpu.get_barrier_semaphore()
    for p in range(1, half):
        peer = lax.rem(chip + p, half) * 2 + par
        pl.semaphore_signal(barrier, inc=1, device_id={"row": peer}, device_id_type=MESH)
    pl.semaphore_signal(barrier, inc=1, device_id={"row": sib}, device_id_type=MESH)
    for p in range(1, ncol):
        pl.semaphore_signal(
            barrier, inc=1, device_id={"col": lax.rem(c + p, ncol)}, device_id_type=MESH
        )
    snd[:, :width] = nodes_ref[...]
    lane = lax.broadcasted_iota(jnp.int32, (rows, LANES), 1)
    tail = jnp.zeros((rows, LANES), F32)
    for k in range(3):
        tail = jnp.where(lane == k, column(ints_ref[k : k + 1, :].astype(F32)), tail)
    snd[:, width:] = tail.astype(BF)
    pl.semaphore_wait(barrier, half + ncol - 1)

    def direct(p):
        peer = lax.rem(chip + p, half) * 2 + par
        return pltpu.make_async_remote_copy(
            src_ref=snd,
            dst_ref=rbuf.at[slot],
            send_sem=dsend.at[p],
            recv_sem=recv.at[slot],
            device_id={"row": peer},
            device_id_type=MESH,
        )

    def forward(k):
        s = 2 * k + par
        return pltpu.make_async_remote_copy(
            src_ref=rbuf.at[s],
            dst_ref=rbuf.at[s],
            send_sem=fsend.at[k],
            recv_sem=recv.at[s],
            device_id={"row": sib},
            device_id_type=MESH,
        )

    def arrived(s):
        return pltpu.make_async_remote_copy(
            src_ref=rbuf.at[s],
            dst_ref=rbuf.at[s],
            send_sem=fsend.at[0],
            recv_sem=recv.at[s],
            device_id={"row": sib},
            device_id_type=MESH,
        )

    @pl.when(is_src)
    def _():
        for p in range(1, half):
            direct(p).start()
        rbuf[slot] = snd[...]

    mask = jnp.where(
        lax.broadcasted_iota(jnp.int32, (heads, width), 1) // hsize
        == lax.broadcasted_iota(jnp.int32, (heads, width), 0),
        1.0,
        0.0,
    )
    pgain = column(pgain_ref[...])
    egain = column(egain_ref[...])
    cpad = -(-classes // 16) * 16
    rel = jnp.concatenate([rel_ref[...], jnp.zeros((heads, cpad - classes), F32)], axis=1)
    rel_hi = rel.astype(BF)
    rel_lo = (rel - rel_hi.astype(F32)).astype(BF)
    rel_cat = jnp.concatenate([rel_hi.astype(F32), rel_lo.astype(F32)], axis=1).astype(BF)

    def wide_rows(b, base, n):
        return jnp.concatenate(
            [
                zs[b, t, pl.ds(base + u, chans, stride=IB), :]
                for u in range(n)
                for t in range(nl)
            ],
            axis=1,
        )

    def spread(b):
        pair_in(b).wait()
        for t in range(nl):
            zs[b, t] = (
                pin[b, :, :, t * LANES : (t + 1) * LANES].astype(F32).reshape(chans * IB, LANES)
            )

    def bias_block(b):
        spread(b)

        def chunk(k, carry):
            base = k * NA
            pnorm = chan_norm(wide_rows(b, base, NA), pgain)
            bg = jnp.dot(wbg_ref[...], pnorm, preferred_element_type=F32)
            sg = 0.5 * jnp.tanh(0.5 * bg[heads:]) + 0.5
            for u in range(NA):
                at = pl.ds(pl.multiple_of((b * IB + base + u) * heads, heads), heads)
                bias_s[at, :] = bg[:heads, u * cols : (u + 1) * cols]
                sig_s[at, :] = sg[:, u * cols : (u + 1) * cols]
            return carry

        lax.fori_loop(0, IB // NA, chunk, 0)

    for b in range(nblk - 1):
        bias_block(b)
    for k in range(npc // 2):
        mine = c * npc + 2 * k + par == r

        @pl.when(jnp.logical_not(mine))
        def _():
            arrived(2 * k + par).wait_recv()

        forward(k).start()
    bias_block(nblk - 1)

    wq_copy.wait()
    own = node_norm(nodes_ref[...].astype(F32), ngain_ref[...])
    query = jnp.dot(own, wqkv[:, :width], preferred_element_type=F32)
    qf[...] = 0.25 * query.astype(BF).astype(F32)
    for k in range(npc // 2):
        arrived(2 * k + 1 - par).wait_recv()
    for s in range(npc):
        normed = node_norm(rbuf[s, :, :width].astype(F32), ngain_ref[...])
        kv = jnp.dot(normed, wqkv[:, width:], preferred_element_type=F32).astype(BF)
        key[s * rows : (s + 1) * rows, :] = kv[:, :width]
        val[s * rows : (s + 1) * rows, :] = kv[:, width:]
    tails = jnp.concatenate([rbuf[s, :, width:] for s in range(npc)], axis=0)
    pick = jnp.where(
        lax.broadcasted_iota(jnp.int32, (8, LANES), 0)
        == lax.broadcasted_iota(jnp.int32, (8, LANES), 1),
        1.0,
        0.0,
    ).astype(BF)
    col_ints = lax.dot_general(
        pick, tails, (((1,), (1,)), ((), ())), preferred_element_type=F32
    )
    chain_c = col_ints[0:1].astype(jnp.int32)
    res_c = col_ints[1:2].astype(jnp.int32)
    valid = jnp.where(col_ints[2:3] == 1.0, 1.0, 0.0)
    class_ids = lax.broadcasted_iota(jnp.int32, (cpad, cols), 0)

    def attend(k, carry):
        base = pl.multiple_of(k * NC, NC)
        at = pl.ds(pl.multiple_of(base * heads, NC * heads), NC * heads)
        rels = []
        for u in range(NC):
            qb[u * heads : (u + 1) * heads, :] = (qf[pl.ds(base + u, 1), :] * mask).astype(BF)
            gi = base + u
            offset = jnp.clip(res_s[gi] - res_c, -radius, radius) + radius
            cls = jnp.where(chain_c == chain_s[gi], offset, 2 * radius + 1)
            hot = jnp.where(class_ids == cls, 1.0, 0.0).astype(BF)
            rels.append(
                jnp.dot(
                    rel_cat, jnp.concatenate([hot, hot], axis=0), preferred_element_type=F32
                )
            )
        scores = lax.dot_general(
            qb[...], key[...], (((1,), (1,)), ((), ())), preferred_element_type=F32
        )
        logits = jnp.clip(scores + bias_s[at, :] + jnp.concatenate(rels, axis=0), -5.0, 5.0)
        lg_s[at, :] = logits.astype(BF)
        weights = jnp.exp(logits) * valid
        gated = (weights * sig_s[at, :]).astype(BF)
        full = jnp.dot(gated, val[...], preferred_element_type=F32)
        dsum = jnp.sum(weights, axis=1, keepdims=True)
        nd[pl.ds(base, NC), :width] = jnp.sum(full.reshape(NC, heads, width) * mask[None], axis=1)
        nd[pl.ds(base, NC), width:] = jnp.sum(dsum.reshape(NC, heads, 1) * mask[None], axis=1)
        return carry

    lax.fori_loop(0, rows // NC, attend, 0)

    def exchange(p):
        return pltpu.make_async_remote_copy(
            src_ref=nd,
            dst_ref=xbuf.at[p - 1],
            send_sem=xsend.at[p - 1],
            recv_sem=xrecv.at[p - 1],
            device_id={"col": lax.rem(c + p, ncol)},
            device_id_type=MESH,
        )

    for p in range(1, ncol):
        exchange(p).start()

    win = (0.5 * win_ref[...].astype(F32)).astype(BF)

    def mlp_block(b, carry):
        def chunk(k, carry):
            base = k * ND
            z = wide_rows(b, base, ND)
            lg = jnp.concatenate(
                [
                    lg_s[
                        pl.ds(pl.multiple_of((b * IB + base + u) * heads, heads), heads), :
                    ]
                    for u in range(ND)
                ],
                axis=1,
            )
            first = z + jnp.dot(wedge_ref[...], lg, preferred_element_type=F32)
            enorm = chan_norm(first, egain)
            y = jnp.dot(win, enorm, preferred_element_type=F32)
            arg = y * (GELU_A + GELU_B * (y * y))
            hidden = (y + y * jnp.tanh(arg)).astype(BF)
            res = first + jnp.dot(wout_ref[...], hidden, preferred_element_type=F32)
            for u in range(ND):
                for t in range(nl):
                    at = u * cols + t * LANES
                    os[t, pl.ds(base + u, chans, stride=IB), :] = res[:, at : at + LANES]
            return carry

        lax.fori_loop(0, IB // ND, chunk, 0)
        for t in range(nl):
            pout[b, :, :, t * LANES : (t + 1) * LANES] = (
                os[t].reshape(chans, IB, LANES).astype(BF)
            )
        pair_outc(b).start()
        return carry

    lax.fori_loop(0, nblk, mlp_block, 0)

    total = nd[...]
    for p in range(1, ncol):
        exchange(p).wait_recv()
        total = total + xbuf[p - 1]
    attended = (total[:, :width] / total[:, width:]).astype(BF)
    wo_copy.wait()
    node_out[...] = jnp.dot(attended, wo[...], preferred_element_type=F32).astype(BF)

    for p in range(1, ncol):
        exchange(p).wait_send()

    @pl.when(is_src)
    def _():
        for p in range(1, half):
            direct(p).wait_send()

    for k in range(npc // 2):
        forward(k).wait_send()
    for b in range(nblk):
        pair_outc(b).wait()


def body(
    nrow,
    ncol,
    nodes,
    chain_ids,
    residue_index,
    pad_mask,
    pairs,
    node_gain,
    w_qkv,
    w_out,
    pair_gain,
    w_bias_gate,
    rel_table,
    w_edge,
    edge_norm_gain,
    w_mlp_in,
    w_mlp_out,
):
    rows, width = nodes.shape
    chans, _, cols = pairs.shape
    heads = rel_table.shape[0]
    npc = cols // rows
    nblk = rows // IB
    nl = cols // LANES
    ints = jnp.stack([chain_ids, residue_index, pad_mask], axis=0)
    vm = pl.BlockSpec(memory_space=pltpu.VMEM)
    sm = pl.BlockSpec(memory_space=pltpu.SMEM)
    hb = pl.BlockSpec(memory_space=pl.ANY)
    dma = pltpu.SemaphoreType.DMA
    return pl.pallas_call(
        functools.partial(fused_kernel, nrow, ncol),
        in_specs=[sm, sm, vm, vm, hb, hb, hb] + [vm] * 8,
        out_specs=[vm, hb],
        out_shape=[
            jax.ShapeDtypeStruct((rows, width), BF),
            jax.ShapeDtypeStruct((chans, rows, cols), BF),
        ],
        scratch_shapes=[
            pltpu.VMEM((rows, width + LANES), BF),
            pltpu.VMEM((npc, rows, width + LANES), BF),
            pltpu.VMEM(w_qkv.shape, BF),
            pltpu.VMEM(w_out.shape, BF),
            pltpu.VMEM((nblk, chans, IB, cols), BF),
            pltpu.VMEM((nblk, chans, IB, cols), BF),
            pltpu.VMEM((nblk, nl, chans * IB, LANES), F32),
            pltpu.VMEM((nl, chans * IB, LANES), F32),
            pltpu.VMEM((rows * heads, cols), F32),
            pltpu.VMEM((rows * heads, cols), F32),
            pltpu.VMEM((rows * heads, cols), BF),
            pltpu.VMEM((rows, width), F32),
            pltpu.VMEM((cols, width), BF),
            pltpu.VMEM((cols, width), BF),
            pltpu.VMEM((NC * heads, width), BF),
            pltpu.VMEM((rows, 2 * width), F32),
            pltpu.VMEM((ncol - 1, rows, 2 * width), F32),
            dma((nblk,)),
            dma((nblk,)),
            dma((2,)),
            dma((nrow // 2,)),
            dma((npc // 2,)),
            dma((npc,)),
            dma((ncol - 1,)),
            dma((ncol - 1,)),
        ],
        compiler_params=pltpu.CompilerParams(
            vmem_limit_bytes=60 << 20, collective_id=0, has_side_effects=True
        ),
        name="fused_layer",
    )(
        chain_ids,
        residue_index,
        ints,
        nodes,
        pairs,
        w_qkv,
        w_out,
        node_gain[None],
        pair_gain[None],
        edge_norm_gain[None],
        w_bias_gate,
        rel_table,
        w_edge,
        w_mlp_in,
        w_mlp_out,
    )


def solution(mesh):
    split = P(("groups", "row"))
    in_specs = (
        P(("groups", "row"), None),
        split,
        split,
        split,
        P(None, ("groups", "row"), "col"),
    ) + (P(),) * 10
    out_specs = (P(("groups", "row"), None), P(None, ("groups", "row"), "col"))
    return jax.shard_map(
        functools.partial(body, mesh.shape["row"], mesh.shape["col"]),
        mesh=mesh,
        in_specs=in_specs,
        out_specs=out_specs,
        check_vma=False,
    )
```

```python
import functools
import jax
import jax.numpy as jnp
from jax import lax
from jax.experimental import pallas as pl
from jax.experimental.pallas import tpu as pltpu
from jax.sharding import PartitionSpec as P

IB = 16
NA = 4
NC = 8
ND = 4
GELU_A = 2.0 * (2.0 / 3.141592653589793) ** 0.5
GELU_B = GELU_A * 4.0 * 0.044715
MESH = pl.DeviceIdType.MESH
BF, F32 = jnp.bfloat16, jnp.float32
LANES = 128


def node_norm(values, gain):
    mean = jnp.mean(values, axis=1, keepdims=True)
    cent = values - mean
    var = jnp.mean(cent * cent, axis=1, keepdims=True)
    return (cent * lax.rsqrt(var + 1e-05) * gain).astype(BF)


def chan_norm(values, gain):
    inv = 1.0 / values.shape[0]
    mean = jnp.sum(values, axis=0, keepdims=True) * inv
    cent = values - mean
    var = jnp.sum(cent * cent, axis=0, keepdims=True) * inv
    return (cent * lax.rsqrt(var + 1e-05) * gain).astype(BF)


def column(row):
    n = row.shape[1]
    eye = lax.broadcasted_iota(jnp.int32, (n, n), 0) == lax.broadcasted_iota(jnp.int32, (n, n), 1)
    return jnp.sum(jnp.where(eye, row, 0.0), axis=1, keepdims=True)


def flip(mat):
    n = mat.shape[0]
    eye = jnp.where(
        lax.broadcasted_iota(jnp.int32, (n, n), 0) == lax.broadcasted_iota(jnp.int32, (n, n), 1),
        1.0,
        0.0,
    ).astype(BF)
    return lax.dot_general(
        mat, eye, (((0,), (0,)), ((), ())), preferred_element_type=F32
    ).astype(BF)


def fused_kernel(
    nrow,
    ncol,
    chain_s,
    res_s,
    chain_ref,
    res_ref,
    pad_ref,
    nodes_ref,
    pairs_hbm,
    wqkv_hbm,
    wo_hbm,
    ngain_ref,
    pgain_ref,
    egain_ref,
    wbg_ref,
    rel_ref,
    wedge_ref,
    win_ref,
    wout_ref,
    node_out,
    pairs_out,
    snd,
    gbuf,
    hbuf,
    sbuf,
    nbuf,
    wqkv,
    wo,
    pin,
    pout,
    zs,
    os,
    bias_s,
    sig_s,
    lg_s,
    qf,
    key,
    val,
    qb,
    nd,
    xbuf,
    pin_sem,
    pout_sem,
    w_sem,
    dsend,
    drecv,
    hsend,
    hrecv,
    ssem,
    xsend,
    xrecv,
):
    rows, width = nodes_ref.shape
    chans = wbg_ref.shape[0]
    heads, classes = rel_ref.shape
    cols = key.shape[0]
    hsize = width // heads
    radius = (classes - 2) // 2
    npc = cols // rows
    nblk = rows // IB
    nl = cols // LANES
    half = nrow // 2
    r = lax.axis_index("row")
    c = lax.axis_index("col")
    par = lax.rem(r, 2)
    sib = r + 1 - 2 * par
    chip = r // 2
    h2 = npc // 2
    prow = rows // ncol

    def pair_in(b):
        return pltpu.make_async_copy(
            pairs_hbm.at[:, pl.ds(b * IB, IB), :], pin.at[b], pin_sem.at[b]
        )

    def pair_outc(b):
        return pltpu.make_async_copy(
            pout.at[b], pairs_out.at[:, pl.ds(b * IB, IB), :], pout_sem.at[b]
        )

    wq_copy = pltpu.make_async_copy(wqkv_hbm, wqkv, w_sem.at[0])
    wo_copy = pltpu.make_async_copy(wo_hbm, wo, w_sem.at[1])
    for b in range(nblk):
        pair_in(b).start()
    wq_copy.start()
    wo_copy.start()

    barrier = pltpu.get_barrier_semaphore()
    for p in range(1, half):
        peer = lax.rem(chip + p, half) * 2 + par
        pl.semaphore_signal(barrier, inc=1, device_id={"row": peer}, device_id_type=MESH)
    pl.semaphore_signal(barrier, inc=1, device_id={"row": sib}, device_id_type=MESH)
    for p in range(1, ncol):
        pl.semaphore_signal(
            barrier, inc=1, device_id={"col": lax.rem(c + p, ncol)}, device_id_type=MESH
        )
    snd[:, :width] = nodes_ref[...]
    lane = lax.broadcasted_iota(jnp.int32, (rows, LANES), 1)
    tail = jnp.zeros((rows, LANES), F32)
    for k, ref in enumerate((chain_ref, res_ref, pad_ref)):
        tail = jnp.where(lane == k, column(ref[...].astype(F32)), tail)
    snd[:, width:] = tail.astype(BF)
    pl.semaphore_wait(barrier, half + ncol - 1)

    def direct(p):
        peer = lax.rem(chip + p, half) * 2 + par
        return pltpu.make_async_remote_copy(
            src_ref=gbuf.at[chip],
            dst_ref=gbuf.at[chip],
            send_sem=dsend.at[p],
            recv_sem=drecv.at[chip],
            device_id={"row": peer},
            device_id_type=MESH,
        )

    def direct_in(p):
        j = lax.rem(chip + p, half)
        return pltpu.make_async_remote_copy(
            src_ref=gbuf.at[j],
            dst_ref=gbuf.at[j],
            send_sem=dsend.at[p],
            recv_sem=drecv.at[j],
            device_id={"row": j * 2 + par},
            device_id_type=MESH,
        )

    def across(p):
        c2 = lax.rem(c + p, ncol)
        return pltpu.make_async_remote_copy(
            src_ref=gbuf.at[pl.ds(c2 * h2, h2)],
            dst_ref=hbuf.at[c],
            send_sem=hsend.at[p],
            recv_sem=hrecv.at[c],
            device_id={"col": c2},
            device_id_type=MESH,
        )

    def across_in(p):
        c2 = lax.rem(c + p, ncol)
        return pltpu.make_async_remote_copy(
            src_ref=gbuf.at[pl.ds(c2 * h2, h2)],
            dst_ref=hbuf.at[c2],
            send_sem=hsend.at[p],
            recv_sem=hrecv.at[c2],
            device_id={"col": c2},
            device_id_type=MESH,
        )

    twin = pltpu.make_async_remote_copy(
        src_ref=hbuf,
        dst_ref=sbuf,
        send_sem=ssem.at[0],
        recv_sem=ssem.at[1],
        device_id={"row": sib},
        device_id_type=MESH,
    )

    gbuf[chip] = snd[pl.ds(pl.multiple_of(c * prow, prow), prow), :]
    for p in range(1, half):
        direct(p).start()

    mask = jnp.where(
        lax.broadcasted_iota(jnp.int32, (heads, width), 1) // hsize
        == lax.broadcasted_iota(jnp.int32, (heads, width), 0),
        1.0,
        0.0,
    )
    ngain = jnp.concatenate([ngain_ref[k : k + 1, :] for k in range(width // LANES)], axis=1)
    wbg = flip(wbg_ref[...])
    wedge = flip(wedge_ref[...])
    win = (0.5 * flip(win_ref[...]).astype(F32)).astype(BF)
    pgain = column(pgain_ref[...])
    egain = column(egain_ref[...])
    cpad = -(-classes // 16) * 16
    rel = jnp.concatenate([rel_ref[...], jnp.zeros((heads, cpad - classes), F32)], axis=1)
    rel_hi = rel.astype(BF)
    rel_lo = (rel - rel_hi.astype(F32)).astype(BF)
    rel_cat = jnp.concatenate([rel_hi.astype(F32), rel_lo.astype(F32)], axis=1).astype(BF)

    def wide_rows(b, base, n):
        return jnp.concatenate(
            [
                zs[b, t, pl.ds(base + u, chans, stride=IB), :]
                for u in range(n)
                for t in range(nl)
            ],
            axis=1,
        )

    def spread(b):
        pair_in(b).wait()
        for t in range(nl):
            zs[b, t] = (
                pin[b, :, :, t * LANES : (t + 1) * LANES].astype(F32).reshape(chans * IB, LANES)
            )

    def bias_block(b):
        spread(b)

        def chunk(k, carry):
            base = k * NA
            pnorm = chan_norm(wide_rows(b, base, NA), pgain)
            bg = jnp.dot(wbg, pnorm, preferred_element_type=F32)
            sg = 0.5 * jnp.tanh(0.5 * bg[heads:]) + 0.5
            for u in range(NA):
                at = pl.ds(pl.multiple_of((b * IB + base + u) * heads, heads), heads)
                bias_s[at, :] = bg[:heads, u * cols : (u + 1) * cols]
                sig_s[at, :] = sg[:, u * cols : (u + 1) * cols]
            return carry

        lax.fori_loop(0, IB // NA, chunk, 0)

    for b in range(nblk - 1):
        bias_block(b)
    for p in range(1, half):
        direct_in(p).wait_recv()
    for p in range(1, ncol):
        across(p).start()
    hbuf[c] = gbuf[pl.ds(c * h2, h2)]
    bias_block(nblk - 1)
    for p in range(1, ncol):
        across_in(p).wait_recv()
    twin.start()
    wq_copy.wait()
    own = node_norm(nodes_ref[...].astype(F32), ngain)
    query = jnp.dot(own, wqkv[:, :width], preferred_element_type=F32)
    qf[...] = 0.25 * query.astype(BF).astype(F32)
    twin.wait_recv()
    for k in range(h2):
        for q in range(ncol):
            at = (2 * k + par) * rows + q * prow
            nbuf[pl.ds(pl.multiple_of(at, prow), prow), :] = hbuf[q, k]
            at = (2 * k + 1 - par) * rows + q * prow
            nbuf[pl.ds(pl.multiple_of(at, prow), prow), :] = sbuf[q, k]
    normed = node_norm(nbuf[:, :width].astype(F32), ngain)
    key[...] = jnp.dot(
        normed, wqkv[:, width : 2 * width], preferred_element_type=F32
    ).astype(BF)
    val[...] = jnp.dot(normed, wqkv[:, 2 * width :], preferred_element_type=F32).astype(BF)
    tails = nbuf[:, width:]
    pick = jnp.where(
        lax.broadcasted_iota(jnp.int32, (8, LANES), 0)
        == lax.broadcasted_iota(jnp.int32, (8, LANES), 1),
        1.0,
        0.0,
    ).astype(BF)
    col_ints = lax.dot_general(
        pick, tails, (((1,), (1,)), ((), ())), preferred_element_type=F32
    )
    chain_c = col_ints[0:1].astype(jnp.int32)
    res_c = col_ints[1:2].astype(jnp.int32)
    valid = jnp.where(col_ints[2:3] == 1.0, 1.0, 0.0)
    class_ids = lax.broadcasted_iota(jnp.int32, (cpad, cols), 0)

    emask = jnp.where(
        lax.broadcasted_iota(jnp.int32, (heads, LANES), 0)
        == lax.broadcasted_iota(jnp.int32, (heads, LANES), 1),
        1.0,
        0.0,
    )

    def exchange(p, k):
        at = pl.ds(pl.multiple_of(k * NC, NC), NC)
        return pltpu.make_async_remote_copy(
            src_ref=nd.at[at],
            dst_ref=xbuf.at[p - 1, at],
            send_sem=xsend.at[p - 1, k],
            recv_sem=xrecv.at[p - 1, k],
            device_id={"col": lax.rem(c + p, ncol)},
            device_id_type=MESH,
        )

    def attend(k, carry):
        base = pl.multiple_of(k * NC, NC)
        at = pl.ds(pl.multiple_of(base * heads, NC * heads), NC * heads)
        rels = []
        for u in range(NC):
            qb[u * heads : (u + 1) * heads, :] = (qf[pl.ds(base + u, 1), :] * mask).astype(BF)
            gi = base + u
            offset = jnp.clip(res_s[gi] - res_c, -radius, radius) + radius
            cls = jnp.where(chain_c == chain_s[gi], offset, 2 * radius + 1)
            hot = jnp.where(class_ids == cls, 1.0, 0.0).astype(BF)
            rels.append(
                jnp.dot(
                    rel_cat, jnp.concatenate([hot, hot], axis=0), preferred_element_type=F32
                )
            )
        scores = lax.dot_general(
            qb[...], key[...], (((1,), (1,)), ((), ())), preferred_element_type=F32
        )
        logits = jnp.clip(scores + bias_s[at, :] + jnp.concatenate(rels, axis=0), -5.0, 5.0)
        lg_s[at, :] = logits.astype(BF)
        weights = jnp.exp(logits) * valid
        gated = (weights * sig_s[at, :]).astype(BF)
        full = jnp.dot(gated, val[...], preferred_element_type=F32)
        dsum = jnp.sum(weights, axis=1, keepdims=True)
        nd[pl.ds(base, NC), :width] = jnp.sum(full.reshape(NC, heads, width) * mask[None], axis=1)
        nd[pl.ds(base, NC), width:] = jnp.sum(dsum.reshape(NC, heads, 1) * emask[None], axis=1)
        for p in range(1, ncol):
            exchange(p, k).start()
        return carry

    lax.fori_loop(0, rows // NC, attend, 0)

    def mlp_block(b, carry):
        def chunk(k, carry):
            base = k * ND
            z = wide_rows(b, base, ND)
            lg = jnp.concatenate(
                [
                    lg_s[
                        pl.ds(pl.multiple_of((b * IB + base + u) * heads, heads), heads), :
                    ]
                    for u in range(ND)
                ],
                axis=1,
            )
            first = z + jnp.dot(wedge, lg, preferred_element_type=F32)
            enorm = chan_norm(first, egain)
            y = jnp.dot(win, enorm, preferred_element_type=F32)
            arg = y * (GELU_A + GELU_B * (y * y))
            hidden = (y + y * jnp.tanh(arg)).astype(BF)
            res = first + jnp.dot(wout_ref[...], hidden, preferred_element_type=F32)
            for u in range(ND):
                for t in range(nl):
                    at = u * cols + t * LANES
                    os[t, pl.ds(base + u, chans, stride=IB), :] = res[:, at : at + LANES]
            return carry

        lax.fori_loop(0, IB // ND, chunk, 0)
        for t in range(nl):
            pout[b, :, :, t * LANES : (t + 1) * LANES] = (
                os[t].reshape(chans, IB, LANES).astype(BF)
            )
        pair_outc(b).start()
        return carry

    lax.fori_loop(0, nblk, mlp_block, 0)

    total = nd[...]
    for p in range(1, ncol):
        for k in range(rows // NC):
            exchange(p, k).wait_recv()
        total = total + xbuf[p - 1]
    expand = jnp.where(
        lax.broadcasted_iota(jnp.int32, (LANES, width), 1) // hsize
        == lax.broadcasted_iota(jnp.int32, (LANES, width), 0),
        1.0,
        0.0,
    )
    denom = jnp.dot(
        total[:, width:],
        expand,
        precision=lax.Precision.HIGHEST,
        preferred_element_type=F32,
    )
    attended = (total[:, :width] / denom).astype(BF)
    wo_copy.wait()
    node_out[...] = jnp.dot(attended, wo[...], preferred_element_type=F32).astype(BF)

    for p in range(1, ncol):
        for k in range(rows // NC):
            exchange(p, k).wait_send()
        across(p).wait_send()
    for p in range(1, half):
        direct(p).wait_send()
    twin.wait_send()
    for b in range(nblk):
        pair_outc(b).wait()


def body(
    nrow,
    ncol,
    nodes,
    chain_ids,
    residue_index,
    pad_mask,
    pairs,
    node_gain,
    w_qkv,
    w_out,
    pair_gain,
    w_bias_gate,
    rel_table,
    w_edge,
    edge_norm_gain,
    w_mlp_in,
    w_mlp_out,
):
    rows, width = nodes.shape
    chans, _, cols = pairs.shape
    heads = rel_table.shape[0]
    npc = cols // rows
    nblk = rows // IB
    nl = cols // LANES
    vm = pl.BlockSpec(memory_space=pltpu.VMEM)
    sm = pl.BlockSpec(memory_space=pltpu.SMEM)
    hb = pl.BlockSpec(memory_space=pl.ANY)
    dma = pltpu.SemaphoreType.DMA
    return pl.pallas_call(
        functools.partial(fused_kernel, nrow, ncol),
        in_specs=[sm, sm, vm, vm, vm, vm, hb, hb, hb] + [vm] * 8,
        out_specs=[vm, hb],
        out_shape=[
            jax.ShapeDtypeStruct((rows, width), BF),
            jax.ShapeDtypeStruct((chans, rows, cols), BF),
        ],
        scratch_shapes=[
            pltpu.VMEM((rows, width + LANES), BF),
            pltpu.VMEM((nrow // 2, rows // ncol, width + LANES), BF),
            pltpu.VMEM((ncol, npc // 2, rows // ncol, width + LANES), BF),
            pltpu.VMEM((ncol, npc // 2, rows // ncol, width + LANES), BF),
            pltpu.VMEM((cols, width + LANES), BF),
            pltpu.VMEM(w_qkv.shape, BF),
            pltpu.VMEM(w_out.shape, BF),
            pltpu.VMEM((nblk, chans, IB, cols), BF),
            pltpu.VMEM((nblk, chans, IB, cols), BF),
            pltpu.VMEM((nblk, nl, chans * IB, LANES), F32),
            pltpu.VMEM((nl, chans * IB, LANES), F32),
            pltpu.VMEM((rows * heads, cols), F32),
            pltpu.VMEM((rows * heads, cols), F32),
            pltpu.VMEM((rows * heads, cols), BF),
            pltpu.VMEM((rows, width), F32),
            pltpu.VMEM((cols, width), BF),
            pltpu.VMEM((cols, width), BF),
            pltpu.VMEM((NC * heads, width), BF),
            pltpu.VMEM((rows, width + LANES), F32),
            pltpu.VMEM((ncol - 1, rows, width + LANES), F32),
            dma((nblk,)),
            dma((nblk,)),
            dma((2,)),
            dma((nrow // 2,)),
            dma((nrow // 2,)),
            dma((ncol,)),
            dma((ncol,)),
            dma((2,)),
            dma((ncol - 1, rows // NC)),
            dma((ncol - 1, rows // NC)),
        ],
        compiler_params=pltpu.CompilerParams(
            vmem_limit_bytes=60 << 20, collective_id=0, has_side_effects=True
        ),
        name="fused_layer",
    )(
        chain_ids,
        residue_index,
        chain_ids[None],
        residue_index[None],
        pad_mask[None],
        nodes,
        pairs,
        w_qkv,
        w_out,
        node_gain.reshape(width // LANES, LANES),
        pair_gain[None],
        edge_norm_gain[None],
        w_bias_gate.T,
        rel_table,
        w_edge.T,
        w_mlp_in.T,
        w_mlp_out,
    )


def solution(mesh):
    split = P(("groups", "row"))
    in_specs = (
        P(("groups", "row"), None),
        split,
        split,
        split,
        P(None, ("groups", "row"), "col"),
    ) + (P(),) * 10
    out_specs = (P(("groups", "row"), None), P(None, ("groups", "row"), "col"))
    return jax.shard_map(
        functools.partial(body, mesh.shape["row"], mesh.shape["col"]),
        mesh=mesh,
        in_specs=in_specs,
        out_specs=out_specs,
        check_vma=False,
    )
```

```python
import functools
import jax
import jax.numpy as jnp
from jax import lax
from jax.experimental import pallas as pl
from jax.experimental.pallas import tpu as pltpu
from jax.sharding import PartitionSpec as P

IB = 16
NA = 8
NC = 8
ND = 8
GELU_A = 2.0 * (2.0 / 3.141592653589793) ** 0.5
GELU_B = GELU_A * 4.0 * 0.044715
MESH = pl.DeviceIdType.MESH
BF, F32 = jnp.bfloat16, jnp.float32
LANES = 128


def node_norm(values, gain):
    mean = jnp.mean(values, axis=1, keepdims=True)
    cent = values - mean
    var = jnp.mean(cent * cent, axis=1, keepdims=True)
    return (cent * lax.rsqrt(var + 1e-05) * gain).astype(BF)


def chan_norm(values, gain):
    inv = 1.0 / values.shape[0]
    mean = jnp.sum(values, axis=0, keepdims=True) * inv
    cent = values - mean
    var = jnp.sum(cent * cent, axis=0, keepdims=True) * inv
    return (cent * lax.rsqrt(var + 1e-05) * gain).astype(BF)


def column(row):
    n = row.shape[1]
    eye = lax.broadcasted_iota(jnp.int32, (n, n), 0) == lax.broadcasted_iota(jnp.int32, (n, n), 1)
    return jnp.sum(jnp.where(eye, row, 0.0), axis=1, keepdims=True)


def flip(mat):
    n = mat.shape[0]
    eye = jnp.where(
        lax.broadcasted_iota(jnp.int32, (n, n), 0) == lax.broadcasted_iota(jnp.int32, (n, n), 1),
        1.0,
        0.0,
    ).astype(BF)
    return lax.dot_general(
        mat, eye, (((0,), (0,)), ((), ())), preferred_element_type=F32
    ).astype(BF)


def fused_kernel(
    nrow,
    ncol,
    chain_s,
    res_s,
    chain_ref,
    res_ref,
    pad_ref,
    nodes_ref,
    pairs_hbm,
    wqkv_hbm,
    wo_hbm,
    ngain_ref,
    pgain_ref,
    egain_ref,
    wbg_ref,
    rel_ref,
    wedge_ref,
    win_ref,
    wout_ref,
    node_out,
    pairs_out,
    snd,
    gbuf,
    hbuf,
    sbuf,
    nbuf,
    wqkv,
    wo,
    pin,
    pout,
    zs,
    os,
    bias_s,
    sig_s,
    lg_s,
    qf,
    key,
    val,
    qb,
    nd,
    xbuf,
    pin_sem,
    pout_sem,
    w_sem,
    dsend,
    drecv,
    hsend,
    hrecv,
    ssem,
    xsend,
    xrecv,
):
    rows, width = nodes_ref.shape
    chans = wbg_ref.shape[0]
    heads, classes = rel_ref.shape
    cols = key.shape[0]
    hsize = width // heads
    radius = (classes - 2) // 2
    npc = cols // rows
    nblk = rows // IB
    nl = cols // LANES
    half = nrow // 2
    r = lax.axis_index("row")
    c = lax.axis_index("col")
    par = lax.rem(r, 2)
    sib = r + 1 - 2 * par
    chip = r // 2
    h2 = npc // 2
    prow = rows // ncol

    def pair_in(b):
        return pltpu.make_async_copy(
            pairs_hbm.at[:, pl.ds(b * IB, IB), :], pin.at[b], pin_sem.at[b]
        )

    def pair_outc(b):
        return pltpu.make_async_copy(
            pout.at[b], pairs_out.at[:, pl.ds(b * IB, IB), :], pout_sem.at[b]
        )

    wq_copy = pltpu.make_async_copy(wqkv_hbm, wqkv, w_sem.at[0])
    wo_copy = pltpu.make_async_copy(wo_hbm, wo, w_sem.at[1])
    for b in range(nblk):
        pair_in(b).start()
    wq_copy.start()
    wo_copy.start()

    barrier = pltpu.get_barrier_semaphore()
    for p in range(1, half):
        peer = lax.rem(chip + p, half) * 2 + par
        pl.semaphore_signal(barrier, inc=1, device_id={"row": peer}, device_id_type=MESH)
    pl.semaphore_signal(barrier, inc=1, device_id={"row": sib}, device_id_type=MESH)
    for p in range(1, ncol):
        pl.semaphore_signal(
            barrier, inc=1, device_id={"col": lax.rem(c + p, ncol)}, device_id_type=MESH
        )
    snd[:, :width] = nodes_ref[...]
    lane = lax.broadcasted_iota(jnp.int32, (rows, LANES), 1)
    tail = jnp.zeros((rows, LANES), F32)
    for k, ref in enumerate((chain_ref, res_ref, pad_ref)):
        tail = jnp.where(lane == k, column(ref[...].astype(F32)), tail)
    snd[:, width:] = tail.astype(BF)

    def direct(p):
        peer = lax.rem(chip + p, half) * 2 + par
        return pltpu.make_async_remote_copy(
            src_ref=gbuf.at[chip],
            dst_ref=gbuf.at[chip],
            send_sem=dsend.at[p],
            recv_sem=drecv.at[chip],
            device_id={"row": peer},
            device_id_type=MESH,
        )

    def direct_in(p):
        j = lax.rem(chip + p, half)
        return pltpu.make_async_remote_copy(
            src_ref=gbuf.at[j],
            dst_ref=gbuf.at[j],
            send_sem=dsend.at[p],
            recv_sem=drecv.at[j],
            device_id={"row": j * 2 + par},
            device_id_type=MESH,
        )

    def across(p):
        c2 = lax.rem(c + p, ncol)
        return pltpu.make_async_remote_copy(
            src_ref=gbuf.at[pl.ds(c2 * h2, h2)],
            dst_ref=hbuf.at[c],
            send_sem=hsend.at[p],
            recv_sem=hrecv.at[c],
            device_id={"col": c2},
            device_id_type=MESH,
        )

    def across_in(p):
        c2 = lax.rem(c + p, ncol)
        return pltpu.make_async_remote_copy(
            src_ref=gbuf.at[pl.ds(c2 * h2, h2)],
            dst_ref=hbuf.at[c2],
            send_sem=hsend.at[p],
            recv_sem=hrecv.at[c2],
            device_id={"col": c2},
            device_id_type=MESH,
        )

    twin = pltpu.make_async_remote_copy(
        src_ref=hbuf,
        dst_ref=sbuf,
        send_sem=ssem.at[0],
        recv_sem=ssem.at[1],
        device_id={"row": sib},
        device_id_type=MESH,
    )

    gbuf[chip] = snd[pl.ds(pl.multiple_of(c * prow, prow), prow), :]
    pl.semaphore_wait(barrier, half + ncol - 1)
    for p in range(1, half):
        direct(p).start()
    mask = jnp.where(
        lax.broadcasted_iota(jnp.int32, (heads, width), 1) // hsize
        == lax.broadcasted_iota(jnp.int32, (heads, width), 0),
        1.0,
        0.0,
    )
    ngain = jnp.concatenate([ngain_ref[k : k + 1, :] for k in range(width // LANES)], axis=1)
    wbg = flip(wbg_ref[...])
    wedge = flip(wedge_ref[...])
    win = (0.5 * flip(win_ref[...]).astype(F32)).astype(BF)
    pgain = column(pgain_ref[...])
    egain = column(egain_ref[...])
    cpad = -(-classes // 16) * 16
    rel = jnp.concatenate([rel_ref[...], jnp.zeros((heads, cpad - classes), F32)], axis=1)
    rel_hi = rel.astype(BF)
    rel_lo = (rel - rel_hi.astype(F32)).astype(BF)
    rel_cat = jnp.concatenate([rel_hi.astype(F32), rel_lo.astype(F32)], axis=1).astype(BF)

    def wide_rows(b, base, n):
        return jnp.concatenate(
            [
                zs[b, t, pl.ds(base + u, chans, stride=IB), :]
                for u in range(n)
                for t in range(nl)
            ],
            axis=1,
        )

    def spread(b):
        pair_in(b).wait()
        for t in range(nl):
            zs[b, t] = (
                pin[b, :, :, t * LANES : (t + 1) * LANES].astype(F32).reshape(chans * IB, LANES)
            )

    def bias_block(b):
        spread(b)

        def chunk(k, carry):
            base = k * NA
            pnorm = chan_norm(wide_rows(b, base, NA), pgain)
            bg = jnp.dot(wbg, pnorm, preferred_element_type=F32)
            sg = 0.5 * jnp.tanh(0.5 * bg[heads:]) + 0.5
            for u in range(NA):
                at = pl.ds(pl.multiple_of((b * IB + base + u) * heads, heads), heads)
                bias_s[at, :] = bg[:heads, u * cols : (u + 1) * cols]
                sig_s[at, :] = sg[:, u * cols : (u + 1) * cols]
            return carry

        lax.fori_loop(0, IB // NA, chunk, 0)

    for b in range(nblk - 1):
        bias_block(b)
    wq_copy.wait()
    own = node_norm(nodes_ref[...].astype(F32), ngain)
    query = jnp.dot(own, wqkv[:, :width], preferred_element_type=F32)
    qf[...] = 0.25 * query.astype(BF).astype(F32)
    for p in range(1, half):
        direct_in(p).wait_recv()
    for p in range(1, ncol):
        across(p).start()
    hbuf[c] = gbuf[pl.ds(c * h2, h2)]
    bias_block(nblk - 1)
    for p in range(1, ncol):
        across_in(p).wait_recv()
    twin.start()
    twin.wait_recv()
    for k in range(h2):
        for q in range(ncol):
            at = (2 * k + par) * rows + q * prow
            nbuf[pl.ds(pl.multiple_of(at, prow), prow), :] = hbuf[q, k]
            at = (2 * k + 1 - par) * rows + q * prow
            nbuf[pl.ds(pl.multiple_of(at, prow), prow), :] = sbuf[q, k]
    normed = node_norm(nbuf[:, :width].astype(F32), ngain)
    key[...] = jnp.dot(
        normed, wqkv[:, width : 2 * width], preferred_element_type=F32
    ).astype(BF)
    val[...] = jnp.dot(normed, wqkv[:, 2 * width :], preferred_element_type=F32).astype(BF)
    tails = nbuf[:, width:]
    pick = jnp.where(
        lax.broadcasted_iota(jnp.int32, (8, LANES), 0)
        == lax.broadcasted_iota(jnp.int32, (8, LANES), 1),
        1.0,
        0.0,
    ).astype(BF)
    col_ints = lax.dot_general(
        pick, tails, (((1,), (1,)), ((), ())), preferred_element_type=F32
    )
    chain_c = col_ints[0:1].astype(jnp.int32)
    res_c = col_ints[1:2].astype(jnp.int32)
    valid = jnp.where(col_ints[2:3] == 1.0, 1.0, 0.0)
    class_ids = lax.broadcasted_iota(jnp.int32, (cpad, cols), 0)

    emask = jnp.where(
        lax.broadcasted_iota(jnp.int32, (heads, LANES), 0)
        == lax.broadcasted_iota(jnp.int32, (heads, LANES), 1),
        1.0,
        0.0,
    )

    def exchange(p, k):
        at = pl.ds(pl.multiple_of(k * NC, NC), NC)
        return pltpu.make_async_remote_copy(
            src_ref=nd.at[at],
            dst_ref=xbuf.at[p - 1, at],
            send_sem=xsend.at[p - 1, k],
            recv_sem=xrecv.at[p - 1, k],
            device_id={"col": lax.rem(c + p, ncol)},
            device_id_type=MESH,
        )

    def attend(k, carry):
        base = pl.multiple_of(k * NC, NC)
        at = pl.ds(pl.multiple_of(base * heads, NC * heads), NC * heads)
        rels = []
        for u in range(NC):
            qb[u * heads : (u + 1) * heads, :] = (qf[pl.ds(base + u, 1), :] * mask).astype(BF)
            gi = base + u
            offset = jnp.clip(res_s[gi] - res_c, -radius, radius) + radius
            cls = jnp.where(chain_c == chain_s[gi], offset, 2 * radius + 1)
            hot = jnp.where(class_ids == cls, 1.0, 0.0).astype(BF)
            rels.append(
                jnp.dot(
                    rel_cat, jnp.concatenate([hot, hot], axis=0), preferred_element_type=F32
                )
            )
        scores = lax.dot_general(
            qb[...], key[...], (((1,), (1,)), ((), ())), preferred_element_type=F32
        )
        logits = jnp.clip(scores + bias_s[at, :] + jnp.concatenate(rels, axis=0), -5.0, 5.0)
        lg_s[at, :] = logits.astype(BF)
        weights = jnp.exp(logits) * valid
        gated = (weights * sig_s[at, :]).astype(BF)
        full = jnp.dot(gated, val[...], preferred_element_type=F32)
        dsum = jnp.sum(weights, axis=1, keepdims=True)
        nd[pl.ds(base, NC), :width] = jnp.sum(full.reshape(NC, heads, width) * mask[None], axis=1)
        nd[pl.ds(base, NC), width:] = jnp.sum(dsum.reshape(NC, heads, 1) * emask[None], axis=1)
        for p in range(1, ncol):
            exchange(p, k).start()
        return carry

    lax.fori_loop(0, rows // NC, attend, 0)

    def mlp_block(b, carry):
        def chunk(k, carry):
            base = k * ND
            z = wide_rows(b, base, ND)
            lg = jnp.concatenate(
                [
                    lg_s[
                        pl.ds(pl.multiple_of((b * IB + base + u) * heads, heads), heads), :
                    ]
                    for u in range(ND)
                ],
                axis=1,
            )
            first = z + jnp.dot(wedge, lg, preferred_element_type=F32)
            enorm = chan_norm(first, egain)
            y = jnp.dot(win, enorm, preferred_element_type=F32)
            arg = y * (GELU_A + GELU_B * (y * y))
            hidden = (y + y * jnp.tanh(arg)).astype(BF)
            res = first + jnp.dot(wout_ref[...], hidden, preferred_element_type=F32)
            for u in range(ND):
                for t in range(nl):
                    at = u * cols + t * LANES
                    os[t, pl.ds(base + u, chans, stride=IB), :] = res[:, at : at + LANES]
            return carry

        lax.fori_loop(0, IB // ND, chunk, 0)
        for t in range(nl):
            pout[b, :, :, t * LANES : (t + 1) * LANES] = (
                os[t].reshape(chans, IB, LANES).astype(BF)
            )
        pair_outc(b).start()
        return carry

    lax.fori_loop(0, nblk, mlp_block, 0)

    total = nd[...]
    for p in range(1, ncol):
        for k in range(rows // NC):
            exchange(p, k).wait_recv()
        total = total + xbuf[p - 1]
    expand = jnp.where(
        lax.broadcasted_iota(jnp.int32, (LANES, width), 1) // hsize
        == lax.broadcasted_iota(jnp.int32, (LANES, width), 0),
        1.0,
        0.0,
    )
    denom = jnp.dot(
        total[:, width:],
        expand,
        precision=lax.Precision.HIGHEST,
        preferred_element_type=F32,
    )
    attended = (total[:, :width] / denom).astype(BF)
    wo_copy.wait()
    node_out[...] = jnp.dot(attended, wo[...], preferred_element_type=F32).astype(BF)

    for p in range(1, ncol):
        for k in range(rows // NC):
            exchange(p, k).wait_send()
        across(p).wait_send()
    for p in range(1, half):
        direct(p).wait_send()
    twin.wait_send()
    for b in range(nblk):
        pair_outc(b).wait()


def body(
    nrow,
    ncol,
    nodes,
    chain_ids,
    residue_index,
    pad_mask,
    pairs,
    node_gain,
    w_qkv,
    w_out,
    pair_gain,
    w_bias_gate,
    rel_table,
    w_edge,
    edge_norm_gain,
    w_mlp_in,
    w_mlp_out,
):
    rows, width = nodes.shape
    chans, _, cols = pairs.shape
    heads = rel_table.shape[0]
    npc = cols // rows
    nblk = rows // IB
    nl = cols // LANES
    vm = pl.BlockSpec(memory_space=pltpu.VMEM)
    sm = pl.BlockSpec(memory_space=pltpu.SMEM)
    hb = pl.BlockSpec(memory_space=pl.ANY)
    dma = pltpu.SemaphoreType.DMA
    return pl.pallas_call(
        functools.partial(fused_kernel, nrow, ncol),
        in_specs=[sm, sm, vm, vm, vm, vm, hb, hb, hb] + [vm] * 8,
        out_specs=[vm, hb],
        out_shape=[
            jax.ShapeDtypeStruct((rows, width), BF),
            jax.ShapeDtypeStruct((chans, rows, cols), BF),
        ],
        scratch_shapes=[
            pltpu.VMEM((rows, width + LANES), BF),
            pltpu.VMEM((nrow // 2, rows // ncol, width + LANES), BF),
            pltpu.VMEM((ncol, npc // 2, rows // ncol, width + LANES), BF),
            pltpu.VMEM((ncol, npc // 2, rows // ncol, width + LANES), BF),
            pltpu.VMEM((cols, width + LANES), BF),
            pltpu.VMEM(w_qkv.shape, BF),
            pltpu.VMEM(w_out.shape, BF),
            pltpu.VMEM((nblk, chans, IB, cols), BF),
            pltpu.VMEM((nblk, chans, IB, cols), BF),
            pltpu.VMEM((nblk, nl, chans * IB, LANES), F32),
            pltpu.VMEM((nl, chans * IB, LANES), F32),
            pltpu.VMEM((rows * heads, cols), F32),
            pltpu.VMEM((rows * heads, cols), F32),
            pltpu.VMEM((rows * heads, cols), BF),
            pltpu.VMEM((rows, width), F32),
            pltpu.VMEM((cols, width), BF),
            pltpu.VMEM((cols, width), BF),
            pltpu.VMEM((NC * heads, width), BF),
            pltpu.VMEM((rows, width + LANES), F32),
            pltpu.VMEM((ncol - 1, rows, width + LANES), F32),
            dma((nblk,)),
            dma((nblk,)),
            dma((2,)),
            dma((nrow // 2,)),
            dma((nrow // 2,)),
            dma((ncol,)),
            dma((ncol,)),
            dma((2,)),
            dma((ncol - 1, rows // NC)),
            dma((ncol - 1, rows // NC)),
        ],
        compiler_params=pltpu.CompilerParams(
            vmem_limit_bytes=60 << 20, collective_id=0, has_side_effects=True
        ),
        name="fused_layer",
    )(
        chain_ids,
        residue_index,
        chain_ids[None],
        residue_index[None],
        pad_mask[None],
        nodes,
        pairs,
        w_qkv,
        w_out,
        node_gain.reshape(width // LANES, LANES),
        pair_gain[None],
        edge_norm_gain[None],
        w_bias_gate.T,
        rel_table,
        w_edge.T,
        w_mlp_in.T,
        w_mlp_out,
    )


def solution(mesh):
    split = P(("groups", "row"))
    in_specs = (
        P(("groups", "row"), None),
        split,
        split,
        split,
        P(None, ("groups", "row"), "col"),
    ) + (P(),) * 10
    out_specs = (P(("groups", "row"), None), P(None, ("groups", "row"), "col"))
    return jax.shard_map(
        functools.partial(body, mesh.shape["row"], mesh.shape["col"]),
        mesh=mesh,
        in_specs=in_specs,
        out_specs=out_specs,
        check_vma=False,
    )
```

```python
import functools
import jax
import jax.numpy as jnp
from jax import lax
from jax.experimental import pallas as pl
from jax.experimental.pallas import tpu as pltpu
from jax.sharding import PartitionSpec as P

IB = 16
NA = 8
NC = 16
ND = 8
GELU_A = 2.0 * (2.0 / 3.141592653589793) ** 0.5
GELU_B = GELU_A * 4.0 * 0.044715
MESH = pl.DeviceIdType.MESH
BF, F32 = jnp.bfloat16, jnp.float32
LANES = 128


def node_norm(values, gain):
    mean = jnp.mean(values, axis=1, keepdims=True)
    cent = values - mean
    var = jnp.mean(cent * cent, axis=1, keepdims=True)
    return (cent * lax.rsqrt(var + 1e-05) * gain).astype(BF)


def chan_norm(values, gain):
    inv = 1.0 / values.shape[0]
    mean = jnp.sum(values, axis=0, keepdims=True) * inv
    cent = values - mean
    var = jnp.sum(cent * cent, axis=0, keepdims=True) * inv
    return (cent * lax.rsqrt(var + 1e-05) * gain).astype(BF)


def column(row):
    n = row.shape[1]
    eye = lax.broadcasted_iota(jnp.int32, (n, n), 0) == lax.broadcasted_iota(jnp.int32, (n, n), 1)
    return jnp.sum(jnp.where(eye, row, 0.0), axis=1, keepdims=True)


def flip(mat):
    n = mat.shape[0]
    eye = jnp.where(
        lax.broadcasted_iota(jnp.int32, (n, n), 0) == lax.broadcasted_iota(jnp.int32, (n, n), 1),
        1.0,
        0.0,
    ).astype(BF)
    return lax.dot_general(
        mat, eye, (((0,), (0,)), ((), ())), preferred_element_type=F32
    ).astype(BF)


def fused_kernel(
    nrow,
    ncol,
    chain_s,
    res_s,
    chain_ref,
    res_ref,
    pad_ref,
    nodes_ref,
    pairs_hbm,
    wqkv_hbm,
    wo_hbm,
    ngain_ref,
    pgain_ref,
    egain_ref,
    wbg_ref,
    rel_ref,
    wedge_ref,
    win_ref,
    wout_ref,
    node_out,
    pairs_out,
    snd,
    gbuf,
    hbuf,
    sbuf,
    nbuf,
    wqkv,
    wo,
    pin,
    pout,
    zs,
    os,
    bias_s,
    sig_s,
    lg_s,
    qf,
    key,
    val,
    qb,
    nd,
    xbuf,
    pin_sem,
    pout_sem,
    w_sem,
    dsend,
    drecv,
    hsend,
    hrecv,
    ssem,
    xsend,
    xrecv,
):
    rows, width = nodes_ref.shape
    chans = wbg_ref.shape[0]
    heads, classes = rel_ref.shape
    cols = key.shape[0]
    hsize = width // heads
    radius = (classes - 2) // 2
    npc = cols // rows
    nblk = rows // IB
    nl = cols // LANES
    half = nrow // 2
    r = lax.axis_index("row")
    c = lax.axis_index("col")
    par = lax.rem(r, 2)
    sib = r + 1 - 2 * par
    chip = r // 2
    h2 = npc // 2
    prow = rows // ncol

    def pair_in(b):
        return pltpu.make_async_copy(
            pairs_hbm.at[:, pl.ds(b * IB, IB), :], pin.at[b], pin_sem.at[b]
        )

    def pair_outc(b):
        return pltpu.make_async_copy(
            pout.at[b], pairs_out.at[:, pl.ds(b * IB, IB), :], pout_sem.at[b]
        )

    wq_copy = pltpu.make_async_copy(wqkv_hbm, wqkv, w_sem.at[0])
    wo_copy = pltpu.make_async_copy(wo_hbm, wo, w_sem.at[1])
    for b in range(nblk):
        pair_in(b).start()
    wq_copy.start()
    wo_copy.start()

    barrier = pltpu.get_barrier_semaphore()
    for p in range(1, half):
        peer = lax.rem(chip + p, half) * 2 + par
        pl.semaphore_signal(barrier, inc=1, device_id={"row": peer}, device_id_type=MESH)
    pl.semaphore_signal(barrier, inc=1, device_id={"row": sib}, device_id_type=MESH)
    for p in range(1, ncol):
        pl.semaphore_signal(
            barrier, inc=1, device_id={"col": lax.rem(c + p, ncol)}, device_id_type=MESH
        )
    snd[:, :width] = nodes_ref[...]
    lane = lax.broadcasted_iota(jnp.int32, (rows, LANES), 1)
    tail = jnp.zeros((rows, LANES), F32)
    for k, ref in enumerate((chain_ref, res_ref, pad_ref)):
        tail = jnp.where(lane == k, column(ref[...].astype(F32)), tail)
    snd[:, width:] = tail.astype(BF)

    def direct(p):
        peer = lax.rem(chip + p, half) * 2 + par
        return pltpu.make_async_remote_copy(
            src_ref=gbuf.at[chip],
            dst_ref=gbuf.at[chip],
            send_sem=dsend.at[p],
            recv_sem=drecv.at[chip],
            device_id={"row": peer},
            device_id_type=MESH,
        )

    def direct_in(p):
        j = lax.rem(chip + p, half)
        return pltpu.make_async_remote_copy(
            src_ref=gbuf.at[j],
            dst_ref=gbuf.at[j],
            send_sem=dsend.at[p],
            recv_sem=drecv.at[j],
            device_id={"row": j * 2 + par},
            device_id_type=MESH,
        )

    def across(p):
        c2 = lax.rem(c + p, ncol)
        return pltpu.make_async_remote_copy(
            src_ref=gbuf.at[pl.ds(c2 * h2, h2)],
            dst_ref=hbuf.at[c],
            send_sem=hsend.at[p],
            recv_sem=hrecv.at[c],
            device_id={"col": c2},
            device_id_type=MESH,
        )

    def across_in(p):
        c2 = lax.rem(c + p, ncol)
        return pltpu.make_async_remote_copy(
            src_ref=gbuf.at[pl.ds(c2 * h2, h2)],
            dst_ref=hbuf.at[c2],
            send_sem=hsend.at[p],
            recv_sem=hrecv.at[c2],
            device_id={"col": c2},
            device_id_type=MESH,
        )

    twin = pltpu.make_async_remote_copy(
        src_ref=hbuf,
        dst_ref=sbuf,
        send_sem=ssem.at[0],
        recv_sem=ssem.at[1],
        device_id={"row": sib},
        device_id_type=MESH,
    )

    gbuf[chip] = snd[pl.ds(pl.multiple_of(c * prow, prow), prow), :]
    pl.semaphore_wait(barrier, half + ncol - 1)
    for p in range(1, half):
        direct(p).start()
    mask = jnp.where(
        lax.broadcasted_iota(jnp.int32, (heads, width), 1) // hsize
        == lax.broadcasted_iota(jnp.int32, (heads, width), 0),
        1.0,
        0.0,
    )
    ngain = jnp.concatenate([ngain_ref[k : k + 1, :] for k in range(width // LANES)], axis=1)
    wbg = flip(wbg_ref[...])
    wedge = flip(wedge_ref[...])
    win = (0.5 * flip(win_ref[...]).astype(F32)).astype(BF)
    pgain = column(pgain_ref[...])
    egain = column(egain_ref[...])
    cpad = -(-classes // 16) * 16
    rel = jnp.concatenate([rel_ref[...], jnp.zeros((heads, cpad - classes), F32)], axis=1)
    rel_hi = rel.astype(BF)
    rel_lo = (rel - rel_hi.astype(F32)).astype(BF)
    rel_cat = jnp.concatenate([rel_hi.astype(F32), rel_lo.astype(F32)], axis=1).astype(BF)

    def wide_rows(b, base, n):
        return jnp.concatenate(
            [
                zs[b, t, pl.ds(base + u, chans, stride=IB), :]
                for u in range(n)
                for t in range(nl)
            ],
            axis=1,
        )

    def spread(b):
        pair_in(b).wait()
        for t in range(nl):
            zs[b, t] = (
                pin[b, :, :, t * LANES : (t + 1) * LANES].astype(F32).reshape(chans * IB, LANES)
            )

    def bias_block(b):
        spread(b)

        def chunk(k, carry):
            base = k * NA
            pnorm = chan_norm(wide_rows(b, base, NA), pgain)
            bg = jnp.dot(wbg, pnorm, preferred_element_type=F32)
            sg = 0.5 * jnp.tanh(0.5 * bg[heads:]) + 0.5
            for u in range(NA):
                at = pl.ds(pl.multiple_of((b * IB + base + u) * heads, heads), heads)
                bias_s[at, :] = bg[:heads, u * cols : (u + 1) * cols]
                sig_s[at, :] = sg[:, u * cols : (u + 1) * cols]
            return carry

        lax.fori_loop(0, IB // NA, chunk, 0)

    for b in range(nblk - 1):
        bias_block(b)
    wq_copy.wait()
    own = node_norm(nodes_ref[...].astype(F32), ngain)
    query = jnp.dot(own, wqkv[:, :width], preferred_element_type=F32)
    qf[...] = 0.25 * query.astype(BF).astype(F32)
    for p in range(1, half):
        direct_in(p).wait_recv()
    for p in range(1, ncol):
        across(p).start()
    hbuf[c] = gbuf[pl.ds(c * h2, h2)]
    bias_block(nblk - 1)
    for p in range(1, ncol):
        across_in(p).wait_recv()
    twin.start()
    twin.wait_recv()
    for k in range(h2):
        for q in range(ncol):
            at = (2 * k + par) * rows + q * prow
            nbuf[pl.ds(pl.multiple_of(at, prow), prow), :] = hbuf[q, k]
            at = (2 * k + 1 - par) * rows + q * prow
            nbuf[pl.ds(pl.multiple_of(at, prow), prow), :] = sbuf[q, k]
    normed = node_norm(nbuf[:, :width].astype(F32), ngain)
    key[...] = jnp.dot(
        normed, wqkv[:, width : 2 * width], preferred_element_type=F32
    ).astype(BF)
    val[...] = jnp.dot(normed, wqkv[:, 2 * width :], preferred_element_type=F32).astype(BF)
    tails = nbuf[:, width:]
    pick = jnp.where(
        lax.broadcasted_iota(jnp.int32, (8, LANES), 0)
        == lax.broadcasted_iota(jnp.int32, (8, LANES), 1),
        1.0,
        0.0,
    ).astype(BF)
    col_ints = lax.dot_general(
        pick, tails, (((1,), (1,)), ((), ())), preferred_element_type=F32
    )
    chain_c = col_ints[0:1].astype(jnp.int32)
    res_c = col_ints[1:2].astype(jnp.int32)
    valid = jnp.where(col_ints[2:3] == 1.0, 1.0, 0.0)
    class_ids = lax.broadcasted_iota(jnp.int32, (cpad, cols), 0)

    emask = jnp.where(
        lax.broadcasted_iota(jnp.int32, (heads, LANES), 0)
        == lax.broadcasted_iota(jnp.int32, (heads, LANES), 1),
        1.0,
        0.0,
    )

    def exchange(p, k):
        at = pl.ds(pl.multiple_of(k * NC, NC), NC)
        return pltpu.make_async_remote_copy(
            src_ref=nd.at[at],
            dst_ref=xbuf.at[p - 1, at],
            send_sem=xsend.at[p - 1, k],
            recv_sem=xrecv.at[p - 1, k],
            device_id={"col": lax.rem(c + p, ncol)},
            device_id_type=MESH,
        )

    def attend(k, carry):
        base = pl.multiple_of(k * NC, NC)
        at = pl.ds(pl.multiple_of(base * heads, NC * heads), NC * heads)
        rels = []
        for u in range(NC):
            qb[u * heads : (u + 1) * heads, :] = (qf[pl.ds(base + u, 1), :] * mask).astype(BF)
            gi = base + u
            offset = jnp.clip(res_s[gi] - res_c, -radius, radius) + radius
            cls = jnp.where(chain_c == chain_s[gi], offset, 2 * radius + 1)
            hot = jnp.where(class_ids == cls, 1.0, 0.0).astype(BF)
            rels.append(
                jnp.dot(
                    rel_cat, jnp.concatenate([hot, hot], axis=0), preferred_element_type=F32
                )
            )
        scores = lax.dot_general(
            qb[...], key[...], (((1,), (1,)), ((), ())), preferred_element_type=F32
        )
        logits = jnp.clip(scores + bias_s[at, :] + jnp.concatenate(rels, axis=0), -5.0, 5.0)
        lg_s[at, :] = logits.astype(BF)
        weights = jnp.exp(logits) * valid
        gated = (weights * sig_s[at, :]).astype(BF)
        full = jnp.dot(gated, val[...], preferred_element_type=F32)
        dsum = jnp.sum(weights, axis=1, keepdims=True)
        nd[pl.ds(base, NC), :width] = jnp.sum(full.reshape(NC, heads, width) * mask[None], axis=1)
        nd[pl.ds(base, NC), width:] = jnp.sum(dsum.reshape(NC, heads, 1) * emask[None], axis=1)
        for p in range(1, ncol):
            exchange(p, k).start()
        return carry

    lax.fori_loop(0, rows // NC, attend, 0)

    def mlp_block(b, carry):
        def chunk(k, carry):
            base = k * ND
            z = wide_rows(b, base, ND)
            lg = jnp.concatenate(
                [
                    lg_s[
                        pl.ds(pl.multiple_of((b * IB + base + u) * heads, heads), heads), :
                    ]
                    for u in range(ND)
                ],
                axis=1,
            )
            first = z + jnp.dot(wedge, lg, preferred_element_type=F32)
            enorm = chan_norm(first, egain)
            y = jnp.dot(win, enorm, preferred_element_type=F32)
            arg = y * (GELU_A + GELU_B * (y * y))
            hidden = (y + y * jnp.tanh(arg)).astype(BF)
            res = first + jnp.dot(wout_ref[...], hidden, preferred_element_type=F32)
            for u in range(ND):
                for t in range(nl):
                    at = u * cols + t * LANES
                    os[t, pl.ds(base + u, chans, stride=IB), :] = res[:, at : at + LANES]
            return carry

        lax.fori_loop(0, IB // ND, chunk, 0)
        for t in range(nl):
            pout[b, :, :, t * LANES : (t + 1) * LANES] = (
                os[t].reshape(chans, IB, LANES).astype(BF)
            )
        pair_outc(b).start()
        return carry

    lax.fori_loop(0, nblk, mlp_block, 0)

    total = nd[...]
    for p in range(1, ncol):
        for k in range(rows // NC):
            exchange(p, k).wait_recv()
        total = total + xbuf[p - 1]
    expand = jnp.where(
        lax.broadcasted_iota(jnp.int32, (LANES, width), 1) // hsize
        == lax.broadcasted_iota(jnp.int32, (LANES, width), 0),
        1.0,
        0.0,
    )
    denom = jnp.dot(
        total[:, width:],
        expand,
        precision=lax.Precision.HIGHEST,
        preferred_element_type=F32,
    )
    attended = (total[:, :width] / denom).astype(BF)
    wo_copy.wait()
    node_out[...] = jnp.dot(attended, wo[...], preferred_element_type=F32).astype(BF)

    for p in range(1, ncol):
        for k in range(rows // NC):
            exchange(p, k).wait_send()
        across(p).wait_send()
    for p in range(1, half):
        direct(p).wait_send()
    twin.wait_send()
    for b in range(nblk):
        pair_outc(b).wait()


def body(
    nrow,
    ncol,
    nodes,
    chain_ids,
    residue_index,
    pad_mask,
    pairs,
    node_gain,
    w_qkv,
    w_out,
    pair_gain,
    w_bias_gate,
    rel_table,
    w_edge,
    edge_norm_gain,
    w_mlp_in,
    w_mlp_out,
):
    rows, width = nodes.shape
    chans, _, cols = pairs.shape
    heads = rel_table.shape[0]
    npc = cols // rows
    nblk = rows // IB
    nl = cols // LANES
    vm = pl.BlockSpec(memory_space=pltpu.VMEM)
    sm = pl.BlockSpec(memory_space=pltpu.SMEM)
    hb = pl.BlockSpec(memory_space=pl.ANY)
    dma = pltpu.SemaphoreType.DMA
    return pl.pallas_call(
        functools.partial(fused_kernel, nrow, ncol),
        in_specs=[sm, sm, vm, vm, vm, vm, hb, hb, hb] + [vm] * 8,
        out_specs=[vm, hb],
        out_shape=[
            jax.ShapeDtypeStruct((rows, width), BF),
            jax.ShapeDtypeStruct((chans, rows, cols), BF),
        ],
        scratch_shapes=[
            pltpu.VMEM((rows, width + LANES), BF),
            pltpu.VMEM((nrow // 2, rows // ncol, width + LANES), BF),
            pltpu.VMEM((ncol, npc // 2, rows // ncol, width + LANES), BF),
            pltpu.VMEM((ncol, npc // 2, rows // ncol, width + LANES), BF),
            pltpu.VMEM((cols, width + LANES), BF),
            pltpu.VMEM(w_qkv.shape, BF),
            pltpu.VMEM(w_out.shape, BF),
            pltpu.VMEM((nblk, chans, IB, cols), BF),
            pltpu.VMEM((nblk, chans, IB, cols), BF),
            pltpu.VMEM((nblk, nl, chans * IB, LANES), F32),
            pltpu.VMEM((nl, chans * IB, LANES), F32),
            pltpu.VMEM((rows * heads, cols), F32),
            pltpu.VMEM((rows * heads, cols), F32),
            pltpu.VMEM((rows * heads, cols), BF),
            pltpu.VMEM((rows, width), F32),
            pltpu.VMEM((cols, width), BF),
            pltpu.VMEM((cols, width), BF),
            pltpu.VMEM((NC * heads, width), BF),
            pltpu.VMEM((rows, width + LANES), F32),
            pltpu.VMEM((ncol - 1, rows, width + LANES), F32),
            dma((nblk,)),
            dma((nblk,)),
            dma((2,)),
            dma((nrow // 2,)),
            dma((nrow // 2,)),
            dma((ncol,)),
            dma((ncol,)),
            dma((2,)),
            dma((ncol - 1, rows // NC)),
            dma((ncol - 1, rows // NC)),
        ],
        compiler_params=pltpu.CompilerParams(
            vmem_limit_bytes=60 << 20, collective_id=0, has_side_effects=True
        ),
        name="fused_layer",
    )(
        chain_ids,
        residue_index,
        chain_ids[None],
        residue_index[None],
        pad_mask[None],
        nodes,
        pairs,
        w_qkv,
        w_out,
        node_gain.reshape(width // LANES, LANES),
        pair_gain[None],
        edge_norm_gain[None],
        w_bias_gate.T,
        rel_table,
        w_edge.T,
        w_mlp_in.T,
        w_mlp_out,
    )


def solution(mesh):
    split = P(("groups", "row"))
    in_specs = (
        P(("groups", "row"), None),
        split,
        split,
        split,
        P(None, ("groups", "row"), "col"),
    ) + (P(),) * 10
    out_specs = (P(("groups", "row"), None), P(None, ("groups", "row"), "col"))
    return jax.shard_map(
        functools.partial(body, mesh.shape["row"], mesh.shape["col"]),
        mesh=mesh,
        in_specs=in_specs,
        out_specs=out_specs,
        check_vma=False,
    )
```
